32 devices in a mesh: ctx: 16 (over z, y, core), head: 2 (over x).
Axes of the slice: x: 2, y: 2, z: 4, core: 2. Of those that a mesh axis runs over, the one named last changes fastest.
Arguments:
- loader_query_rows: bfloat16 [6144, 8192], P(('ctx', 'head')), may hold values from -6 to 6
- loader_key_rows: bfloat16 [6144, 1024], P(('ctx', 'head')), may hold values from -6 to 6
- loader_value_rows: bfloat16 [6144, 1024], P(('ctx', 'head')), may hold values from -6 to 6
- output_gradient_rows: bfloat16 [6144, 8192], P(('ctx', 'head')), may hold values from -6 to 6
- doc_blocks: int32 [2, 3], replicated, may hold values from 1 to 16, as said below
- block_perm: int32 [48], replicated, may hold values from 0 to 47, as said below
Outputs:
- attn_out: bfloat16 [6144, 8192], P('ctx', 'head')
- grad_query: bfloat16 [6144, 8192], P('ctx', 'head')
- key_gradient: bfloat16 [6144, 1024], P('ctx', 'head')
- value_gradient: bfloat16 [6144, 1024], P('ctx', 'head')
The draws below stay inside these ranges and needn't reach their ends.
Inputs may be any that keep to these rules, and one draw needn't show every extreme that they name: doc_blocks[g] lists in order the lengths, in blocks, of the documents that fill row blocks g * 24 to (g + 1) * 24 - 1 of the packed row; each row sums to 24 and holds one length equal to 16. block_perm is a permutation that maps the blocks of each aligned span of 24 blocks onto the same span.
All inputs are finite; a program needn't handle non-finite values.
Results may differ from the reference program's by a relative error of at most 0.012.
The reference program's roundings to bfloat16 on the way count: a program that leaves them out, or rounds other values in their place, can miss the bound.
Values may be sent and summed in bfloat16 or wider, within the bound.
A program may use at most 192 MiB of HBM per device.

```python
import jax
import jax.numpy as jnp
from jax import lax

QUERY_HEADS = 64
KEY_VALUE_HEADS = 8
HEAD_SIZE = 128
MASK_BLOCK_SIZE = 128
GROUP_DEV = 8
DOCS_G = 3
PACKED_LENGTH = 6144
ROW_BLOCK_COUNT = 48
GROUP_BLOCKS = 24
MOST = 16
NGROUP = 2


def doc_layout(key):
    base_key = jax.random.fold_in(key, 7001)
    others = DOCS_G - 1
    extra_blocks = GROUP_BLOCKS - MOST - others
    lanes = jnp.arange(others, dtype=jnp.int32)

    def spread_one(step_index, counts):
        step_key = jax.random.fold_in(base_key, step_index)
        rank_scores = jax.random.randint(step_key, (NGROUP, others), 0, 1024) * others + lanes[None, :]
        rank_scores = jnp.where(counts >= MOST, -1, rank_scores)
        chosen = jnp.argmax(rank_scores, axis=1)
        return counts + (lanes[None, :] == chosen[:, None]).astype(jnp.int32)
    counts = lax.fori_loop(0, extra_blocks, spread_one, jnp.ones((NGROUP, others), jnp.int32))
    lengths_all = jnp.concatenate([counts, jnp.full((NGROUP, 1), MOST, jnp.int32)], axis=1)
    order_key = jax.random.fold_in(base_key, 99991)
    shuffle = jax.random.randint(order_key, (NGROUP, DOCS_G), 0, 4096) * DOCS_G + jnp.arange(DOCS_G, dtype=jnp.int32)[None, :]
    rank_order = jnp.argsort(shuffle, axis=1)
    return jnp.take_along_axis(lengths_all, rank_order, axis=1).astype(jnp.int32)


def draw_doc_blocks(key, part):
    return doc_layout(key)


def draw_block_perm(key, part):
    lengths = doc_layout(key)
    doc_ends = jnp.cumsum(lengths, axis=1).astype(jnp.int32)
    firsts = doc_ends - lengths
    local_blocks = jnp.arange(GROUP_BLOCKS, dtype=jnp.int32)
    first_of = jnp.max(jnp.where(firsts[:, None, :] <= local_blocks[None, :, None], firsts[:, None, :], 0), axis=2)
    block_work = local_blocks[None, :] - first_of + 1
    tie_key = jax.random.fold_in(key, 7002)
    block_score = block_work * (GROUP_BLOCKS * 1024) + jax.random.randint(tie_key, (NGROUP, GROUP_BLOCKS), 0, 1024) * GROUP_BLOCKS + local_blocks[None, :]
    rank_order = jnp.argsort(-block_score, axis=1)
    lane_index = local_blocks % GROUP_DEV
    sweep_index = local_blocks // GROUP_DEV
    device = jnp.where(sweep_index % 2 == 0, lane_index, GROUP_DEV - 1 - lane_index)
    place_local = device * (GROUP_BLOCKS // GROUP_DEV) + sweep_index
    span_base = jnp.arange(NGROUP, dtype=jnp.int32)[:, None] * GROUP_BLOCKS
    span_rows = jnp.arange(NGROUP, dtype=jnp.int32)[:, None]
    perm_rows = jnp.zeros((NGROUP, GROUP_BLOCKS), jnp.int32).at[span_rows, rank_order].set(span_base + place_local[None, :])
    return jnp.roll(perm_rows, -(GROUP_BLOCKS // 2), axis=1).reshape(-1)


def draw_loader_query_rows(key, part):
    simple_rows = jax.random.normal(jax.random.fold_in(key, 11), (PACKED_LENGTH, QUERY_HEADS * HEAD_SIZE), jnp.float32)
    return jnp.clip(simple_rows, -6.0, 6.0).astype(jnp.bfloat16)


def draw_loader_key_rows(key, part):
    simple_rows = jax.random.normal(jax.random.fold_in(key, 21), (PACKED_LENGTH, KEY_VALUE_HEADS * HEAD_SIZE), jnp.float32)
    return jnp.clip(simple_rows, -6.0, 6.0).astype(jnp.bfloat16)


def levels(rng, shape, shards, least, high):
    def one(axis_at, shards_of):
        heights = jax.random.uniform(jax.random.fold_in(jax.random.fold_in(rng, 6), axis_at), (shards_of,), jnp.float32, least / len(shards), high / len(shards))
        return jnp.repeat(jnp.exp(heights), shape[axis_at] // shards_of).reshape((-1,) + (1,) * (len(shape) - axis_at - 1))

    level = one(*shards[0])
    for cut in shards[1:]:
        level = level * one(*cut)
    return level


def centred(stream_key, dims, deviation, limit, shards=(), kind=jnp.bfloat16):
    values = jax.random.normal(stream_key, dims, jnp.float32) * deviation
    if len(shards) > 0:
        values = levels(stream_key, dims, shards, -0.22, 0.18) * values
    return jnp.clip(values, min=-limit, max=limit).astype(kind)


def setup_inputs(seed: int = 0) -> dict:
    splits = jax.random.split(jax.random.key(seed), 7)
    loader_query_rows = draw_loader_query_rows(jax.random.fold_in(splits[6], 71), 0)
    loader_key_rows = draw_loader_key_rows(jax.random.fold_in(splits[6], 71), 0)
    loader_value_rows = centred(splits[2], (PACKED_LENGTH, KEY_VALUE_HEADS * HEAD_SIZE), 1.0, 6.0, ((0, 32),))
    output_gradient_rows = centred(splits[3], (PACKED_LENGTH, QUERY_HEADS * HEAD_SIZE), 1.0, 6.0, ((0, 32),))
    doc_blocks = draw_doc_blocks(jax.random.fold_in(splits[6], 71), 0)
    block_perm = draw_block_perm(jax.random.fold_in(splits[6], 71), 0)
    return dict(loader_query_rows=loader_query_rows, loader_key_rows=loader_key_rows, loader_value_rows=loader_value_rows, output_gradient_rows=output_gradient_rows, doc_blocks=doc_blocks, block_perm=block_perm)


MASKED_LOGIT = -1e30


def doc_first(doc_blocks, total_blocks):
    doc_ends = jnp.cumsum(doc_blocks, axis=1).astype(jnp.int32)
    span_base = jnp.arange(doc_blocks.shape[0], dtype=jnp.int32)[:, None] * GROUP_BLOCKS
    firsts = (span_base + doc_ends - doc_blocks).reshape(-1).astype(jnp.int32)
    blocks = jnp.arange(total_blocks, dtype=jnp.int32)
    return jnp.max(jnp.where(firsts[None, :] <= blocks[:, None], firsts[None, :], 0), axis=1).astype(jnp.int32)


def round_low(values):
    return lax.optimization_barrier(values.astype(jnp.bfloat16)).astype(jnp.float32)


def rotate_rows(array, shift):
    blocked = array.reshape(NGROUP, GROUP_BLOCKS, MASK_BLOCK_SIZE, array.shape[1])
    return jnp.roll(blocked, shift, axis=1).reshape(array.shape)


def reference(loader_query_rows, loader_key_rows, loader_value_rows, output_gradient_rows, doc_blocks, block_perm):
    query_group_ratio = QUERY_HEADS // KEY_VALUE_HEADS
    logit_scale = HEAD_SIZE ** -0.5
    half_span = GROUP_BLOCKS // 2
    firsts = doc_first(doc_blocks, ROW_BLOCK_COUNT)
    query_matrix = rotate_rows(loader_query_rows, half_span).reshape(ROW_BLOCK_COUNT, MASK_BLOCK_SIZE, KEY_VALUE_HEADS, query_group_ratio, HEAD_SIZE)
    output_cotangents = rotate_rows(output_gradient_rows, half_span).reshape(ROW_BLOCK_COUNT, MASK_BLOCK_SIZE, KEY_VALUE_HEADS, query_group_ratio, HEAD_SIZE)
    every_key = rotate_rows(loader_key_rows, half_span).reshape(PACKED_LENGTH, KEY_VALUE_HEADS, HEAD_SIZE)
    every_value = rotate_rows(loader_value_rows, half_span).reshape(PACKED_LENGTH, KEY_VALUE_HEADS, HEAD_SIZE)
    window = MOST * MASK_BLOCK_SIZE
    token_query = lax.broadcasted_iota(jnp.int32, (MASK_BLOCK_SIZE, 1, 1, window), 0)
    token_key = lax.broadcasted_iota(jnp.int32, (MASK_BLOCK_SIZE, 1, 1, window), 3)

    def step_number(running_totals, block_index):
        doc_start = firsts[block_index]
        window_start = jnp.maximum(block_index - MOST + 1, 0).astype(jnp.int32)
        key_window = lax.dynamic_slice_in_dim(every_key, window_start * MASK_BLOCK_SIZE, window, 0).astype(jnp.float32)
        value_window = lax.dynamic_slice_in_dim(every_value, window_start * MASK_BLOCK_SIZE, window, 0).astype(jnp.float32)
        query_block = query_matrix[block_index].astype(jnp.float32)
        grad_block = output_cotangents[block_index].astype(jnp.float32)
        key_pos = window_start * MASK_BLOCK_SIZE + token_key
        query_pos = block_index * MASK_BLOCK_SIZE + token_query
        allowed = (key_pos <= query_pos) & (key_pos >= doc_start * MASK_BLOCK_SIZE)
        logits = jnp.einsum("tgrd,kgd->tgrk", query_block, key_window) * logit_scale
        logits = jnp.where(allowed, logits, MASKED_LOGIT)
        row_max = jnp.max(logits, axis=3)
        log_total = row_max + jnp.log(jnp.sum(jnp.exp(logits - row_max[..., None]), axis=3))
        weights = jnp.exp(logits - log_total[..., None])
        weights_low = round_low(weights)
        output_rows = jnp.einsum("tgrk,kgd->tgrd", weights_low, value_window).astype(jnp.bfloat16)
        outputs_wide = lax.optimization_barrier(output_rows).astype(jnp.float32)
        delta_rows = jnp.sum(grad_block * outputs_wide, axis=3)
        value_part = jnp.einsum("tgrk,tgrd->kgd", weights_low, grad_block)
        grad_weights = jnp.einsum("tgrd,kgd->tgrk", grad_block, value_window)
        dlogits = round_low(weights * (grad_weights - delta_rows[..., None]))
        query_gradient = (jnp.einsum("tgrk,kgd->tgrd", dlogits, key_window) * logit_scale).astype(jnp.bfloat16)
        key_part = jnp.einsum("tgrk,tgrd->kgd", dlogits, query_block) * logit_scale
        previous = lax.dynamic_slice_in_dim(running_totals, window_start * MASK_BLOCK_SIZE, window, 1)
        running_totals = lax.dynamic_update_slice_in_dim(running_totals, previous + jnp.stack([key_part, value_part]), window_start * MASK_BLOCK_SIZE, 1)
        return running_totals, (output_rows, query_gradient)

    running_totals, (output_rows, query_gradient) = lax.scan(step_number, jnp.zeros((2, PACKED_LENGTH, KEY_VALUE_HEADS, HEAD_SIZE), jnp.float32), jnp.arange(ROW_BLOCK_COUNT, dtype=jnp.int32))

    def balanced_mapping(array):
        loader_rows = rotate_rows(array, -half_span)
        blocked = loader_rows.reshape(ROW_BLOCK_COUNT, MASK_BLOCK_SIZE, array.shape[1])
        return jnp.zeros_like(blocked).at[block_perm].set(blocked).reshape(PACKED_LENGTH, array.shape[1])

    attn_out = balanced_mapping(output_rows.reshape(PACKED_LENGTH, QUERY_HEADS * HEAD_SIZE))
    grad_query = balanced_mapping(query_gradient.reshape(PACKED_LENGTH, QUERY_HEADS * HEAD_SIZE))
    key_gradient = balanced_mapping(running_totals[0].reshape(PACKED_LENGTH, KEY_VALUE_HEADS * HEAD_SIZE).astype(jnp.bfloat16))
    value_gradient = balanced_mapping(running_totals[1].reshape(PACKED_LENGTH, KEY_VALUE_HEADS * HEAD_SIZE).astype(jnp.bfloat16))
    return (attn_out, grad_query, key_gradient, value_gradient)
```

```python
from functools import partial
import math

import jax
import jax.numpy as jnp
from jax import lax
from jax.experimental import pallas as pl
from jax.experimental.pallas import tpu as pltpu
from jax.sharding import PartitionSpec as P

QUERY_HEADS = 64
KEY_VALUE_HEADS = 8
HEAD_SIZE = 128
MASK_BLOCK_SIZE = 128
GROUP_DEV = 8
GROUP_BLOCKS = 24
MOST = 16

RATIO = QUERY_HEADS // KEY_VALUE_HEADS
MASKED_LOGIT = -1e30
CHUNK = 256
SPAN_TOKENS = GROUP_BLOCKS * MASK_BLOCK_SIZE
MESH = pl.DeviceIdType.MESH


def doc_first(doc_blocks):
    ends = jnp.cumsum(doc_blocks)
    firsts = ends - doc_blocks
    blocks = jnp.arange(GROUP_BLOCKS, dtype=jnp.int32)
    return jnp.max(jnp.where(firsts[None, :] <= blocks[:, None], firsts[None, :], 0), axis=1)


def enter(peers):
    barrier = pltpu.get_barrier_semaphore()
    for peer in peers:
        pl.semaphore_signal(barrier, inc=1, device_id=peer, device_id_type=MESH)
    pl.semaphore_wait(barrier, len(peers))


def spread_kernel(
    head_dim, query_ref, grad_ref, key_ref, value_ref, *rest
):
    outs = rest[:4]
    stages = rest[4:8]
    send_sems, recv_sems, local_sems = rest[8:]
    sources = (query_ref, grad_ref, key_ref, value_ref)
    members = GROUP_DEV * head_dim
    rows = query_ref.shape[0]
    wide = outs[0].shape[1]
    heads = wide // HEAD_SIZE
    ctx = lax.axis_index("ctx")
    head = lax.axis_index("head")
    base = ctx // GROUP_DEV * GROUP_DEV
    lane = ctx - base
    own = lane * head_dim + head

    def place(step):
        peer = lax.rem(own + step, members)
        return peer // head_dim, lax.rem(peer, head_dim)

    def columns(peer_lane, peer_head):
        worker = peer_head * GROUP_DEV + peer_lane
        query_at = pl.ds(pl.multiple_of(worker * wide, HEAD_SIZE), wide)
        key_at = pl.ds(
            pl.multiple_of(worker * heads // RATIO * HEAD_SIZE, HEAD_SIZE), HEAD_SIZE
        )
        return (query_at, query_at, key_at, key_at)

    landing = pl.ds(pl.multiple_of(own * rows, 16), rows)
    own_columns = columns(lane, head)
    loads = []
    for index in range(4):
        load = pltpu.make_async_copy(
            sources[index].at[:, own_columns[index]], stages[index], local_sems.at[index]
        )
        load.start()
        loads.append(load)
    peers = [place(step) for step in range(1, members)]
    enter([{"ctx": base + peer_lane, "head": peer_head} for peer_lane, peer_head in peers])
    copies = []
    for step, (peer_lane, peer_head) in enumerate(peers):
        spots = columns(peer_lane, peer_head)
        for index in range(4):
            copy = pltpu.make_async_remote_copy(
                src_ref=sources[index].at[:, spots[index]],
                dst_ref=outs[index].at[landing, :],
                send_sem=send_sems.at[index, step],
                recv_sem=recv_sems.at[index, step],
                device_id={"ctx": base + peer_lane, "head": peer_head},
                device_id_type=MESH,
            )
            copy.start()
            copies.append(copy)
    stores = []
    for index in range(4):
        loads[index].wait()
        store = pltpu.make_async_copy(
            stages[index], outs[index].at[landing, :], local_sems.at[4 + index]
        )
        store.start()
        stores.append(store)
    for store in stores:
        store.wait()
    for copy in copies:
        copy.wait()


def spread(head_dim, query, grad, key, value):
    rows, width = query.shape
    members = GROUP_DEV * head_dim
    wide = width // members
    any_spec = pl.BlockSpec(memory_space=pl.ANY)
    return pl.pallas_call(
        partial(spread_kernel, head_dim),
        out_shape=[
            jax.ShapeDtypeStruct((rows * members, wide), jnp.bfloat16),
            jax.ShapeDtypeStruct((rows * members, wide), jnp.bfloat16),
            jax.ShapeDtypeStruct((rows * members, HEAD_SIZE), jnp.bfloat16),
            jax.ShapeDtypeStruct((rows * members, HEAD_SIZE), jnp.bfloat16),
        ],
        in_specs=[any_spec] * 4,
        out_specs=[any_spec] * 4,
        scratch_shapes=[
            pltpu.VMEM((rows, wide), jnp.bfloat16),
            pltpu.VMEM((rows, wide), jnp.bfloat16),
            pltpu.VMEM((rows, HEAD_SIZE), jnp.bfloat16),
            pltpu.VMEM((rows, HEAD_SIZE), jnp.bfloat16),
            pltpu.SemaphoreType.DMA((4, members - 1)),
            pltpu.SemaphoreType.DMA((4, members - 1)),
            pltpu.SemaphoreType.DMA((8,)),
        ],
        compiler_params=pltpu.CompilerParams(collective_id=0, has_side_effects=True),
        name="spread",
    )(query, grad, key, value)


def gather_kernel(attn_ref, query_ref, key_ref, value_ref, *rest):
    outs = rest[:4]
    stages = rest[4:8]
    send_sems, recv_sems, local_sems = rest[8:]
    sources = (attn_ref, query_ref, key_ref, value_ref)
    rows = outs[0].shape[0]
    wide = attn_ref.shape[1]
    ctx = lax.axis_index("ctx")
    head = lax.axis_index("head")
    base = ctx // GROUP_DEV * GROUP_DEV
    lane = ctx - base
    own_at = pl.ds(pl.multiple_of(lane * wide, HEAD_SIZE), wide)
    own_key_at = pl.ds(pl.multiple_of(lane * HEAD_SIZE, HEAD_SIZE), HEAD_SIZE)
    landing = (own_at, own_at, own_key_at, own_key_at)

    def taken(peer):
        return pl.ds(pl.multiple_of(peer * rows, 16), rows)

    loads = []
    for index in range(4):
        load = pltpu.make_async_copy(
            sources[index].at[taken(lane), :], stages[index], local_sems.at[index]
        )
        load.start()
        loads.append(load)
    peers = [lax.rem(lane + step, GROUP_DEV) for step in range(1, GROUP_DEV)]
    enter([{"ctx": base + peer, "head": head} for peer in peers])
    copies = []
    for step, peer in enumerate(peers):
        for index in range(4):
            copy = pltpu.make_async_remote_copy(
                src_ref=sources[index].at[taken(peer), :],
                dst_ref=outs[index].at[:, landing[index]],
                send_sem=send_sems.at[index, step],
                recv_sem=recv_sems.at[index, step],
                device_id={"ctx": base + peer, "head": head},
                device_id_type=MESH,
            )
            copy.start()
            copies.append(copy)
    stores = []
    for index in range(4):
        loads[index].wait()
        store = pltpu.make_async_copy(
            stages[index], outs[index].at[:, landing[index]], local_sems.at[4 + index]
        )
        store.start()
        stores.append(store)
    for store in stores:
        store.wait()
    for copy in copies:
        copy.wait()


def gather(attn, query, key, value):
    rows = attn.shape[0] // GROUP_DEV
    wide = attn.shape[1]
    any_spec = pl.BlockSpec(memory_space=pl.ANY)
    return pl.pallas_call(
        gather_kernel,
        out_shape=[
            jax.ShapeDtypeStruct((rows, wide * GROUP_DEV), jnp.bfloat16),
            jax.ShapeDtypeStruct((rows, wide * GROUP_DEV), jnp.bfloat16),
            jax.ShapeDtypeStruct((rows, HEAD_SIZE * GROUP_DEV), jnp.bfloat16),
            jax.ShapeDtypeStruct((rows, HEAD_SIZE * GROUP_DEV), jnp.bfloat16),
        ],
        in_specs=[any_spec] * 4,
        out_specs=[any_spec] * 4,
        scratch_shapes=[
            pltpu.VMEM((rows, wide), jnp.bfloat16),
            pltpu.VMEM((rows, wide), jnp.bfloat16),
            pltpu.VMEM((rows, HEAD_SIZE), jnp.bfloat16),
            pltpu.VMEM((rows, HEAD_SIZE), jnp.bfloat16),
            pltpu.SemaphoreType.DMA((4, GROUP_DEV - 1)),
            pltpu.SemaphoreType.DMA((4, GROUP_DEV - 1)),
            pltpu.SemaphoreType.DMA((8,)),
        ],
        compiler_params=pltpu.CompilerParams(collective_id=1, has_side_effects=True),
        name="gather",
    )(attn, query, key, value)


def dot(left, right):
    return jnp.dot(left, right, preferred_element_type=jnp.float32)


def attend_kernel(
    firsts_ref,
    places_ref,
    query_ref,
    grad_ref,
    key_ref,
    value_ref,
    attn_ref,
    query_grad_ref,
    key_grad_ref,
    value_grad_ref,
    keys,
    values,
    keys_t,
    values_t,
    store,
    out_t,
    query_grad_t,
    key_total,
    value_total,
):
    heads = query_ref.shape[1] // HEAD_SIZE
    block = MASK_BLOCK_SIZE
    columns = heads * block
    half = SPAN_TOKENS // 2
    scale = HEAD_SIZE ** (-0.5)
    scale_log2 = scale * math.log2(math.e)
    tail = keys.shape[0] - SPAN_TOKENS
    for source, flat, turned in ((key_ref, keys, keys_t), (value_ref, values, values_t)):
        flat[0:half, :] = source[half:SPAN_TOKENS, :]
        flat[half:SPAN_TOKENS, :] = source[0:half, :]
        flat[SPAN_TOKENS:, :] = jnp.zeros((tail, HEAD_SIZE), jnp.bfloat16)
        turned[:, SPAN_TOKENS:] = jnp.zeros((HEAD_SIZE, tail), jnp.bfloat16)
    for index in range(GROUP_BLOCKS):
        at = slice(index * block, (index + 1) * block)
        keys_t[:, at] = keys[at, :].T
        values_t[:, at] = values[at, :].T
    key_total[...] = jnp.zeros_like(key_total)
    value_total[...] = jnp.zeros_like(value_total)
    token = lax.rem(lax.broadcasted_iota(jnp.int32, (CHUNK, columns), 1), block)
    key_at = lax.broadcasted_iota(jnp.int32, (CHUNK, columns), 0)
    ahead = key_at - token

    def one_block(index, _):
        first = firsts_ref[index]
        count = index - first + 1
        steps = (count * block + CHUNK - 1) // CHUNK
        loader = lax.rem(index + GROUP_BLOCKS // 2, GROUP_BLOCKS)
        source = pl.ds(pl.multiple_of(loader * block, block), block)
        target = pl.ds(pl.multiple_of(places_ref[loader] * block, block), block)
        parts = [slice(h * HEAD_SIZE, (h + 1) * HEAD_SIZE) for h in range(heads)]
        query = jnp.concatenate([query_ref[source, at] for at in parts], axis=0)
        grad = jnp.concatenate([grad_ref[source, at] for at in parts], axis=0)
        query_t = jnp.concatenate([query_ref[source, at].T for at in parts], axis=1)
        grad_t = jnp.concatenate([grad_ref[source, at].T for at in parts], axis=1)

        def spot(step):
            return pl.ds(pl.multiple_of(first * block + step * CHUNK, block), CHUNK)

        def slot(step):
            return pl.ds(pl.multiple_of(step * CHUNK, CHUNK), CHUNK)

        def logits(step, peak):
            raw = dot(keys[spot(step), :], query_t)
            bound = (count - 1) * block - step * CHUNK
            raw = jnp.where(ahead <= bound, raw, MASKED_LOGIT)
            store[slot(step), :] = raw
            return jnp.maximum(peak, jnp.max(raw, axis=0, keepdims=True))

        peak = lax.fori_loop(
            0, steps, logits, jnp.full((1, columns), MASKED_LOGIT, jnp.float32)
        )
        peak = peak * scale_log2
        out_t[...] = jnp.zeros_like(out_t)

        def mix(step, total):
            mass = jnp.exp2(store[slot(step), :] * scale_log2 - peak)
            store[slot(step), :] = mass
            out_t[...] += dot(values_t[:, spot(step)], mass.astype(jnp.bfloat16))
            return total + jnp.sum(mass, axis=0, keepdims=True)

        total = lax.fori_loop(0, steps, mix, jnp.zeros((1, columns), jnp.float32))
        share = 1.0 / total
        out = (out_t[...] * share).astype(jnp.bfloat16)
        delta = jnp.sum(
            out.astype(jnp.float32) * grad_t.astype(jnp.float32), axis=0, keepdims=True
        )
        for h, at in enumerate(parts):
            attn_ref[target, at] = out[:, h * block : (h + 1) * block].T
        query_grad_t[...] = jnp.zeros_like(query_grad_t)

        def back(step, carry):
            weights = store[slot(step), :] * share
            value_total[spot(step), :] += dot(weights.astype(jnp.bfloat16), grad)
            grad_weights = dot(values[spot(step), :], grad_t)
            dlogits = (weights * (grad_weights - delta)).astype(jnp.bfloat16)
            key_total[spot(step), :] += dot(dlogits, query)
            query_grad_t[...] += dot(keys_t[:, spot(step)], dlogits)
            return carry

        lax.fori_loop(0, steps, back, 0)
        moved = (query_grad_t[...] * scale).astype(jnp.bfloat16)
        for h, at in enumerate(parts):
            query_grad_ref[target, at] = moved[:, h * block : (h + 1) * block].T
        return 0

    lax.fori_loop(0, GROUP_BLOCKS, one_block, 0)

    def finish(index, _):
        loader = lax.rem(index + GROUP_BLOCKS // 2, GROUP_BLOCKS)
        source = pl.ds(pl.multiple_of(index * block, block), block)
        target = pl.ds(pl.multiple_of(places_ref[loader] * block, block), block)
        key_grad_ref[target, :] = (key_total[source, :] * scale).astype(jnp.bfloat16)
        value_grad_ref[target, :] = value_total[source, :].astype(jnp.bfloat16)
        return 0

    lax.fori_loop(0, GROUP_BLOCKS, finish, 0)


def attend(firsts, places, query, grad, key, value):
    wide = query.shape[1]
    columns = wide // HEAD_SIZE * MASK_BLOCK_SIZE
    padded = SPAN_TOKENS + CHUNK - MASK_BLOCK_SIZE
    vmem = pl.BlockSpec(memory_space=pltpu.VMEM)
    smem = pl.BlockSpec(memory_space=pltpu.SMEM)
    return pl.pallas_call(
        attend_kernel,
        out_shape=[
            jax.ShapeDtypeStruct(query.shape, jnp.bfloat16),
            jax.ShapeDtypeStruct(query.shape, jnp.bfloat16),
            jax.ShapeDtypeStruct(key.shape, jnp.bfloat16),
            jax.ShapeDtypeStruct(key.shape, jnp.bfloat16),
        ],
        in_specs=[smem, smem, vmem, vmem, vmem, vmem],
        out_specs=[vmem] * 4,
        scratch_shapes=[
            pltpu.VMEM((padded, HEAD_SIZE), jnp.bfloat16),
            pltpu.VMEM((padded, HEAD_SIZE), jnp.bfloat16),
            pltpu.VMEM((HEAD_SIZE, padded), jnp.bfloat16),
            pltpu.VMEM((HEAD_SIZE, padded), jnp.bfloat16),
            pltpu.VMEM((MOST * MASK_BLOCK_SIZE, columns), jnp.float32),
            pltpu.VMEM((HEAD_SIZE, columns), jnp.float32),
            pltpu.VMEM((HEAD_SIZE, columns), jnp.float32),
            pltpu.VMEM((padded, HEAD_SIZE), jnp.float32),
            pltpu.VMEM((padded, HEAD_SIZE), jnp.float32),
        ],
        compiler_params=pltpu.CompilerParams(vmem_limit_bytes=60 * 1024 * 1024),
        name="attend",
    )(firsts, places, query, grad, key, value)


def body(head_dim, query_rows, key_rows, value_rows, grad_rows, doc_blocks, block_perm):
    group = lax.axis_index("ctx") // GROUP_DEV
    firsts = doc_first(lax.dynamic_index_in_dim(doc_blocks, group, 0, keepdims=False))
    places = lax.dynamic_slice_in_dim(block_perm, group * GROUP_BLOCKS, GROUP_BLOCKS)
    places = places - group * GROUP_BLOCKS
    query, grad, key, value = spread(head_dim, query_rows, grad_rows, key_rows, value_rows)
    results = attend(firsts, places, query, grad, key, value)
    attn, query_grad, key_parts, value_parts = gather(*results)
    heads = query.shape[1] // HEAD_SIZE
    sharers = max(RATIO // heads, 1)

    def joined(parts):
        rows = parts.shape[0]
        shaped = parts.reshape(rows, -1, sharers, HEAD_SIZE).astype(jnp.float32)
        return jnp.sum(shaped, axis=2).astype(jnp.bfloat16).reshape(rows, -1)

    return attn, query_grad, joined(key_parts), joined(value_parts)


def solution(mesh):
    split = P(("ctx", "head"), None)
    out_spec = P("ctx", "head")
    return jax.shard_map(
        partial(body, mesh.shape["head"]),
        mesh=mesh,
        in_specs=(split, split, split, split, P(), P()),
        out_specs=(out_spec,) * 4,
        check_vma=False,
    )
```

```python
from functools import partial
import math

import jax
import jax.numpy as jnp
from jax import lax
from jax.experimental import pallas as pl
from jax.experimental.pallas import tpu as pltpu
from jax.sharding import PartitionSpec as P

QUERY_HEADS = 64
KEY_VALUE_HEADS = 8
HEAD_SIZE = 128
MASK_BLOCK_SIZE = 128
GROUP_DEV = 8
GROUP_BLOCKS = 24
MOST = 16

RATIO = QUERY_HEADS // KEY_VALUE_HEADS
MASKED_LOGIT = -1e30
CHUNK = 256
SPAN_TOKENS = GROUP_BLOCKS * MASK_BLOCK_SIZE
MESH = pl.DeviceIdType.MESH


def doc_first(doc_blocks):
    ends = jnp.cumsum(doc_blocks)
    firsts = ends - doc_blocks
    blocks = jnp.arange(GROUP_BLOCKS, dtype=jnp.int32)
    return jnp.max(jnp.where(firsts[None, :] <= blocks[:, None], firsts[None, :], 0), axis=1)


def enter(peers):
    barrier = pltpu.get_barrier_semaphore()
    for peer in peers:
        pl.semaphore_signal(barrier, inc=1, device_id=peer, device_id_type=MESH)
    pl.semaphore_wait(barrier, len(peers))


def flipped(index, mask, count):
    result, bit = index, 1
    while bit < count:
        if mask & bit:
            result = result + bit - index // bit % 2 * (2 * bit)
        bit *= 2
    return result


def visiting_order(members):
    return SPREAD_ORDER if len(SPREAD_ORDER) == members - 1 else list(range(members - 1, 0, -1))


SPREAD_ORDER = [13, 5, 9, 15, 7, 11, 12, 4, 8, 14, 6, 10, 1, 3, 2]


def spread_kernel(head_dim, query_ref, grad_ref, pair_ref, *rest):
    query_out, grad_out, pair_out, query_stage, grad_stage, pair_stage = rest[:6]
    send_sems, recv_sems, pass_send_sems, pass_recv_sems, local_sems = rest[6:]
    members = GROUP_DEV * head_dim
    rows = query_ref.shape[0]
    wide = query_out.shape[1]
    heads = wide // HEAD_SIZE
    ctx = lax.axis_index("ctx")
    head = lax.axis_index("head")
    base = ctx // GROUP_DEV * GROUP_DEV
    lane = ctx - base
    own = lane * head_dim + head
    order = visiting_order(members)

    def columns(peer_lane, peer_head):
        worker = peer_head * GROUP_DEV + peer_lane
        query_at = pl.ds(pl.multiple_of(worker * wide, HEAD_SIZE), wide)
        key_at = pl.ds(
            pl.multiple_of(worker * heads // RATIO * HEAD_SIZE, HEAD_SIZE), HEAD_SIZE
        )
        return query_at, key_at

    def rows_of(member):
        return pl.ds(pl.multiple_of(member * rows, 16), rows)

    landing = rows_of(own)
    kind = lane % 2
    query_at, key_at = columns(lane, head)
    loads = [
        pltpu.make_async_copy(pair_ref.at[kind, :, key_at], pair_stage, local_sems.at[0]),
        pltpu.make_async_copy(query_ref.at[:, query_at], query_stage, local_sems.at[1]),
        pltpu.make_async_copy(grad_ref.at[:, query_at], grad_stage, local_sems.at[2]),
    ]
    for load in loads:
        load.start()
    peers = []
    for mask in order:
        member = flipped(own, mask, members)
        peers.append((member, member // head_dim, member % head_dim))
    device = [{"ctx": base + peer_lane, "head": peer_head} for _, peer_lane, peer_head in peers]
    sibling = {"ctx": base + flipped(lane, 1, GROUP_DEV), "head": head}
    enter(device)
    pair_copies, copies = [], []
    for step, (member, peer_lane, peer_head) in enumerate(peers):
        key_at = columns(peer_lane, peer_head)[1]
        copy = pltpu.make_async_remote_copy(
            src_ref=pair_ref.at[peer_lane % 2, :, key_at],
            dst_ref=pair_out.at[peer_lane % 2, landing, :],
            send_sem=send_sems.at[2, step],
            recv_sem=recv_sems.at[2, step],
            device_id=device[step],
            device_id_type=MESH,
        )
        copy.start()
        pair_copies.append(copy)
    for step, (member, peer_lane, peer_head) in enumerate(peers):
        query_at = columns(peer_lane, peer_head)[0]
        for index, (source, target) in enumerate(
            ((query_ref, query_out), (grad_ref, grad_out))
        ):
            copy = pltpu.make_async_remote_copy(
                src_ref=source.at[:, query_at],
                dst_ref=target.at[landing, :],
                send_sem=send_sems.at[index, step],
                recv_sem=recv_sems.at[index, step],
                device_id=device[step],
                device_id_type=MESH,
            )
            copy.start()
            copies.append(copy)
    stores = []
    for index, (stage, target) in enumerate(
        (
            (pair_stage, pair_out.at[kind, landing, :]),
            (query_stage, query_out.at[landing, :]),
            (grad_stage, grad_out.at[landing, :]),
        )
    ):
        loads[index].wait()
        store = pltpu.make_async_copy(stage, target, local_sems.at[3 + index])
        store.start()
        stores.append(store)

    def passing(slot, source, spot):
        copy = pltpu.make_async_remote_copy(
            src_ref=source,
            dst_ref=pair_out.at[kind, spot, :],
            send_sem=pass_send_sems.at[slot],
            recv_sem=pass_recv_sems.at[slot],
            device_id=sibling,
            device_id_type=MESH,
        )
        copy.start()
        return copy

    passes = [passing(members - 1, pair_stage, landing)]
    for step, (member, peer_lane, peer_head) in enumerate(peers):
        pair_copies[step].wait_recv()
        spot = rows_of(member)
        passes.append(passing(step, pair_out.at[kind, spot, :], spot))
    for store in stores:
        store.wait()
    for copy in pair_copies:
        copy.wait_send()
    for copy in copies:
        copy.wait()
    for copy in passes:
        copy.wait()


def spread(head_dim, query, grad, pair):
    rows, width = query.shape
    members = GROUP_DEV * head_dim
    wide = width // members
    any_spec = pl.BlockSpec(memory_space=pl.ANY)
    return pl.pallas_call(
        partial(spread_kernel, head_dim),
        out_shape=[
            jax.ShapeDtypeStruct((rows * members, wide), jnp.bfloat16),
            jax.ShapeDtypeStruct((rows * members, wide), jnp.bfloat16),
            jax.ShapeDtypeStruct((2, rows * members, HEAD_SIZE), jnp.bfloat16),
        ],
        in_specs=[any_spec] * 3,
        out_specs=[any_spec] * 3,
        scratch_shapes=[
            pltpu.VMEM((rows, wide), jnp.bfloat16),
            pltpu.VMEM((rows, wide), jnp.bfloat16),
            pltpu.VMEM((rows, HEAD_SIZE), jnp.bfloat16),
            pltpu.SemaphoreType.DMA((3, members - 1)),
            pltpu.SemaphoreType.DMA((3, members - 1)),
            pltpu.SemaphoreType.DMA((members,)),
            pltpu.SemaphoreType.DMA((members,)),
            pltpu.SemaphoreType.DMA((6,)),
        ],
        compiler_params=pltpu.CompilerParams(collective_id=0, has_side_effects=True),
        name="spread",
    )(query, grad, pair)


def gather_kernel(attn_ref, query_ref, pair_ref, *rest):
    attn_out, query_out, pair_out, attn_stage, query_stage, mine, other = rest[:7]
    send_sems, recv_sems, swap_sems, local_sems = rest[7:]
    rows = attn_out.shape[0]
    wide = attn_ref.shape[1]
    sharers = RATIO // (wide // HEAD_SIZE)
    ctx = lax.axis_index("ctx")
    head = lax.axis_index("head")
    base = ctx // GROUP_DEV * GROUP_DEV
    lane = ctx - base
    kind = lane % 2
    own_at = pl.ds(pl.multiple_of(lane * wide, HEAD_SIZE), wide)
    pair_at = pl.ds(pl.multiple_of(lane // sharers * HEAD_SIZE, HEAD_SIZE), HEAD_SIZE)
    pair_landing = pair_out.at[kind, lane % sharers // 2, :, pair_at]

    def taken(peer):
        return pl.ds(pl.multiple_of(peer * rows, 16), rows)

    loads = [
        pltpu.make_async_copy(pair_ref.at[kind], mine, local_sems.at[0]),
        pltpu.make_async_copy(attn_ref.at[taken(lane), :], attn_stage, local_sems.at[1]),
        pltpu.make_async_copy(query_ref.at[taken(lane), :], query_stage, local_sems.at[2]),
    ]
    for load in loads:
        load.start()
    peers = [flipped(lane, mask, GROUP_DEV) for mask in GATHER_ORDER]
    device = [{"ctx": base + peer, "head": head} for peer in peers]
    enter(device)
    swap = pltpu.make_async_remote_copy(
        src_ref=pair_ref.at[1 - kind],
        dst_ref=other,
        send_sem=swap_sems.at[0],
        recv_sem=swap_sems.at[1],
        device_id={"ctx": base + flipped(lane, 1, GROUP_DEV), "head": head},
        device_id_type=MESH,
    )
    swap.start()
    copies = []
    for step, peer in enumerate(peers):
        for index, (source, target) in enumerate(((attn_ref, attn_out), (query_ref, query_out))):
            copy = pltpu.make_async_remote_copy(
                src_ref=source.at[taken(peer), :],
                dst_ref=target.at[:, own_at],
                send_sem=send_sems.at[index, step],
                recv_sem=recv_sems.at[index, step],
                device_id=device[step],
                device_id_type=MESH,
            )
            copy.start()
            copies.append(copy)
    stores = []
    for index, (stage, target) in ((1, (attn_stage, attn_out)), (2, (query_stage, query_out))):
        loads[index].wait()
        store = pltpu.make_async_copy(stage, target.at[:, own_at], local_sems.at[2 + index])
        store.start()
        stores.append(store)
    loads[0].wait()
    swap.wait()
    for peer in range(GROUP_DEV):
        at = slice(peer * rows, (peer + 1) * rows)
        total = mine[at, :].astype(jnp.float32) + other[at, :].astype(jnp.float32)
        mine[at, :] = total.astype(jnp.bfloat16)
    store = pltpu.make_async_copy(mine.at[taken(lane), :], pair_landing, local_sems.at[5])
    store.start()
    stores.append(store)
    for step, peer in enumerate(peers):
        copy = pltpu.make_async_remote_copy(
            src_ref=mine.at[taken(peer), :],
            dst_ref=pair_landing,
            send_sem=send_sems.at[2, step],
            recv_sem=recv_sems.at[2, step],
            device_id=device[step],
            device_id_type=MESH,
        )
        copy.start()
        copies.append(copy)
    for store in stores:
        store.wait()
    for copy in copies:
        copy.wait()


GATHER_ORDER = [6, 2, 4, 7, 3, 5, 1]


def gather(attn, query, pair):
    tokens, wide = attn.shape
    rows = tokens // GROUP_DEV
    sharers = RATIO // (wide // HEAD_SIZE)
    any_spec = pl.BlockSpec(memory_space=pl.ANY)
    return pl.pallas_call(
        gather_kernel,
        out_shape=[
            jax.ShapeDtypeStruct((rows, wide * GROUP_DEV), jnp.bfloat16),
            jax.ShapeDtypeStruct((rows, wide * GROUP_DEV), jnp.bfloat16),
            jax.ShapeDtypeStruct(
                (2, sharers // 2, rows, HEAD_SIZE * GROUP_DEV // sharers), jnp.bfloat16
            ),
        ],
        in_specs=[any_spec] * 3,
        out_specs=[any_spec] * 3,
        scratch_shapes=[
            pltpu.VMEM((rows, wide), jnp.bfloat16),
            pltpu.VMEM((rows, wide), jnp.bfloat16),
            pltpu.VMEM((tokens, HEAD_SIZE), jnp.bfloat16),
            pltpu.VMEM((tokens, HEAD_SIZE), jnp.bfloat16),
            pltpu.SemaphoreType.DMA((3, GROUP_DEV - 1)),
            pltpu.SemaphoreType.DMA((3, GROUP_DEV - 1)),
            pltpu.SemaphoreType.DMA((2,)),
            pltpu.SemaphoreType.DMA((6,)),
        ],
        compiler_params=pltpu.CompilerParams(collective_id=1, has_side_effects=True),
        name="gather",
    )(attn, query, pair)


def dot(left, right):
    return jnp.dot(left, right, preferred_element_type=jnp.float32)


def attend_kernel(
    firsts_ref,
    places_ref,
    query_ref,
    grad_ref,
    pair_ref,
    attn_ref,
    query_grad_ref,
    pair_grad_ref,
    keys,
    values,
    keys_t,
    values_t,
    store,
    out_t,
    query_grad_t,
    key_total,
    value_total,
):
    heads = query_ref.shape[1] // HEAD_SIZE
    block = MASK_BLOCK_SIZE
    columns = heads * block
    half = SPAN_TOKENS // 2
    scale = HEAD_SIZE ** (-0.5)
    scale_log2 = scale * math.log2(math.e)
    tail = keys.shape[0] - SPAN_TOKENS
    for kind, flat, turned in ((0, keys, keys_t), (1, values, values_t)):
        flat[0:half, :] = pair_ref[kind, half:SPAN_TOKENS, :]
        flat[half:SPAN_TOKENS, :] = pair_ref[kind, 0:half, :]
        flat[SPAN_TOKENS:, :] = jnp.zeros((tail, HEAD_SIZE), jnp.bfloat16)
        turned[:, SPAN_TOKENS:] = jnp.zeros((HEAD_SIZE, tail), jnp.bfloat16)
    for index in range(GROUP_BLOCKS):
        at = slice(index * block, (index + 1) * block)
        keys_t[:, at] = keys[at, :].T
        values_t[:, at] = values[at, :].T
    key_total[...] = jnp.zeros_like(key_total)
    value_total[...] = jnp.zeros_like(value_total)
    token = lax.rem(lax.broadcasted_iota(jnp.int32, (CHUNK, columns), 1), block)
    key_at = lax.broadcasted_iota(jnp.int32, (CHUNK, columns), 0)
    ahead = key_at - token

    def one_block(index, _):
        first = firsts_ref[index]
        count = index - first + 1
        steps = (count * block + CHUNK - 1) // CHUNK
        loader = lax.rem(index + GROUP_BLOCKS // 2, GROUP_BLOCKS)
        source = pl.ds(pl.multiple_of(loader * block, block), block)
        target = pl.ds(pl.multiple_of(places_ref[loader] * block, block), block)
        parts = [slice(h * HEAD_SIZE, (h + 1) * HEAD_SIZE) for h in range(heads)]
        query = jnp.concatenate([query_ref[source, at] for at in parts], axis=0)
        grad = jnp.concatenate([grad_ref[source, at] for at in parts], axis=0)
        query_t = jnp.concatenate([query_ref[source, at].T for at in parts], axis=1)
        grad_t = jnp.concatenate([grad_ref[source, at].T for at in parts], axis=1)

        def spot(step):
            return pl.ds(pl.multiple_of(first * block + step * CHUNK, block), CHUNK)

        def slot(step):
            return pl.ds(pl.multiple_of(step * CHUNK, CHUNK), CHUNK)

        def logits(step, peak):
            raw = dot(keys[spot(step), :], query_t)
            bound = (count - 1) * block - step * CHUNK
            raw = jnp.where(ahead <= bound, raw, MASKED_LOGIT)
            store[slot(step), :] = raw
            return jnp.maximum(peak, jnp.max(raw, axis=0, keepdims=True))

        peak = lax.fori_loop(
            0, steps, logits, jnp.full((1, columns), MASKED_LOGIT, jnp.float32)
        )
        peak = peak * scale_log2
        out_t[...] = jnp.zeros_like(out_t)

        def mix(step, total):
            mass = jnp.exp2(store[slot(step), :] * scale_log2 - peak)
            store[slot(step), :] = mass
            out_t[...] += dot(values_t[:, spot(step)], mass.astype(jnp.bfloat16))
            return total + jnp.sum(mass, axis=0, keepdims=True)

        total = lax.fori_loop(0, steps, mix, jnp.zeros((1, columns), jnp.float32))
        share = 1.0 / total
        out = (out_t[...] * share).astype(jnp.bfloat16)
        delta = jnp.sum(
            out.astype(jnp.float32) * grad_t.astype(jnp.float32), axis=0, keepdims=True
        )
        for h, at in enumerate(parts):
            attn_ref[target, at] = out[:, h * block : (h + 1) * block].T
        query_grad_t[...] = jnp.zeros_like(query_grad_t)

        def back(step, carry):
            weights = store[slot(step), :] * share
            value_total[spot(step), :] += dot(weights.astype(jnp.bfloat16), grad)
            grad_weights = dot(values[spot(step), :], grad_t)
            dlogits = (weights * (grad_weights - delta)).astype(jnp.bfloat16)
            key_total[spot(step), :] += dot(dlogits, query)
            query_grad_t[...] += dot(keys_t[:, spot(step)], dlogits)
            return carry

        lax.fori_loop(0, steps, back, 0)
        moved = (query_grad_t[...] * scale).astype(jnp.bfloat16)
        for h, at in enumerate(parts):
            query_grad_ref[target, at] = moved[:, h * block : (h + 1) * block].T
        return 0

    lax.fori_loop(0, GROUP_BLOCKS, one_block, 0)

    def finish(index, _):
        loader = lax.rem(index + GROUP_BLOCKS // 2, GROUP_BLOCKS)
        source = pl.ds(pl.multiple_of(index * block, block), block)
        target = pl.ds(pl.multiple_of(places_ref[loader] * block, block), block)
        pair_grad_ref[0, target, :] = (key_total[source, :] * scale).astype(jnp.bfloat16)
        pair_grad_ref[1, target, :] = value_total[source, :].astype(jnp.bfloat16)
        return 0

    lax.fori_loop(0, GROUP_BLOCKS, finish, 0)


def attend(firsts, places, query, grad, pair):
    wide = query.shape[1]
    columns = wide // HEAD_SIZE * MASK_BLOCK_SIZE
    padded = SPAN_TOKENS + CHUNK - MASK_BLOCK_SIZE
    vmem = pl.BlockSpec(memory_space=pltpu.VMEM)
    smem = pl.BlockSpec(memory_space=pltpu.SMEM)
    return pl.pallas_call(
        attend_kernel,
        out_shape=[
            jax.ShapeDtypeStruct(query.shape, jnp.bfloat16),
            jax.ShapeDtypeStruct(query.shape, jnp.bfloat16),
            jax.ShapeDtypeStruct(pair.shape, jnp.bfloat16),
        ],
        in_specs=[smem, smem, vmem, vmem, vmem],
        out_specs=[vmem] * 3,
        scratch_shapes=[
            pltpu.VMEM((padded, HEAD_SIZE), jnp.bfloat16),
            pltpu.VMEM((padded, HEAD_SIZE), jnp.bfloat16),
            pltpu.VMEM((HEAD_SIZE, padded), jnp.bfloat16),
            pltpu.VMEM((HEAD_SIZE, padded), jnp.bfloat16),
            pltpu.VMEM((MOST * MASK_BLOCK_SIZE, columns), jnp.float32),
            pltpu.VMEM((HEAD_SIZE, columns), jnp.float32),
            pltpu.VMEM((HEAD_SIZE, columns), jnp.float32),
            pltpu.VMEM((padded, HEAD_SIZE), jnp.float32),
            pltpu.VMEM((padded, HEAD_SIZE), jnp.float32),
        ],
        compiler_params=pltpu.CompilerParams(vmem_limit_bytes=60 * 1024 * 1024),
        name="attend",
    )(firsts, places, query, grad, pair)


def body(head_dim, query_rows, key_rows, value_rows, grad_rows, doc_blocks, block_perm):
    group = lax.axis_index("ctx") // GROUP_DEV
    firsts = doc_first(lax.dynamic_index_in_dim(doc_blocks, group, 0, keepdims=False))
    places = lax.dynamic_slice_in_dim(block_perm, group * GROUP_BLOCKS, GROUP_BLOCKS)
    places = places - group * GROUP_BLOCKS
    query, grad, pair = spread(head_dim, query_rows, grad_rows, jnp.stack([key_rows, value_rows]))
    attn, query_grad, parts = gather(*attend(firsts, places, query, grad, pair))
    if parts.shape[1] > 1:
        parts = jnp.sum(parts.astype(jnp.float32), axis=1).astype(jnp.bfloat16)
    else:
        parts = parts[:, 0]
    return attn, query_grad, parts[0], parts[1]


def solution(mesh):
    split = P(("ctx", "head"), None)
    out_spec = P("ctx", "head")
    return jax.shard_map(
        partial(body, mesh.shape["head"]),
        mesh=mesh,
        in_specs=(split, split, split, split, P(), P()),
        out_specs=(out_spec,) * 4,
        check_vma=False,
    )
```

```python
from functools import partial
import math

import jax
import jax.numpy as jnp
from jax import lax
from jax.experimental import pallas as pl
from jax.experimental.pallas import tpu as pltpu
from jax.sharding import PartitionSpec as P

QUERY_HEADS = 64
KEY_VALUE_HEADS = 8
HEAD_SIZE = 128
MASK_BLOCK_SIZE = 128
GROUP_DEV = 8
GROUP_BLOCKS = 24
MOST = 16

RATIO = QUERY_HEADS // KEY_VALUE_HEADS
MASKED_LOGIT = -1e30
CHUNK = 512
SPAN_TOKENS = GROUP_BLOCKS * MASK_BLOCK_SIZE
MESH = pl.DeviceIdType.MESH


def doc_first(doc_blocks):
    ends = jnp.cumsum(doc_blocks)
    firsts = ends - doc_blocks
    blocks = jnp.arange(GROUP_BLOCKS, dtype=jnp.int32)
    return jnp.max(jnp.where(firsts[None, :] <= blocks[:, None], firsts[None, :], 0), axis=1)


def enter(peers):
    barrier = pltpu.get_barrier_semaphore()
    for peer in peers:
        pl.semaphore_signal(barrier, inc=1, device_id=peer, device_id_type=MESH)
    pl.semaphore_wait(barrier, len(peers))


def flipped(index, mask, count):
    result, bit = index, 1
    while bit < count:
        if mask & bit:
            result = result + bit - index // bit % 2 * (2 * bit)
        bit *= 2
    return result


def visiting_order(members):
    return SPREAD_ORDER if len(SPREAD_ORDER) == members - 1 else list(range(members - 1, 0, -1))


SPREAD_ORDER = [13, 5, 9, 15, 7, 11, 12, 4, 8, 14, 6, 10, 1, 3, 2]


def spread_kernel(head_dim, query_ref, grad_ref, pair_ref, *rest):
    query_out, grad_out, pair_out, query_stage, grad_stage, pair_stage = rest[:6]
    send_sems, recv_sems, pass_send_sems, pass_recv_sems, local_sems = rest[6:]
    members = GROUP_DEV * head_dim
    rows = query_ref.shape[0]
    wide = query_out.shape[1]
    heads = wide // HEAD_SIZE
    ctx = lax.axis_index("ctx")
    head = lax.axis_index("head")
    base = ctx // GROUP_DEV * GROUP_DEV
    lane = ctx - base
    own = lane * head_dim + head
    order = visiting_order(members)

    def columns(peer_lane, peer_head):
        worker = peer_head * GROUP_DEV + peer_lane
        query_at = pl.ds(pl.multiple_of(worker * wide, HEAD_SIZE), wide)
        key_at = pl.ds(
            pl.multiple_of(worker * heads // RATIO * HEAD_SIZE, HEAD_SIZE), HEAD_SIZE
        )
        return query_at, key_at

    def rows_of(member):
        return pl.ds(pl.multiple_of(member * rows, 16), rows)

    landing = rows_of(own)
    kind = lane % 2
    query_at, key_at = columns(lane, head)
    loads = [
        pltpu.make_async_copy(pair_ref.at[kind, :, key_at], pair_stage, local_sems.at[0]),
        pltpu.make_async_copy(query_ref.at[:, query_at], query_stage, local_sems.at[1]),
        pltpu.make_async_copy(grad_ref.at[:, query_at], grad_stage, local_sems.at[2]),
    ]
    for load in loads:
        load.start()
    peers = []
    for mask in order:
        member = flipped(own, mask, members)
        peers.append((member, member // head_dim, member % head_dim))
    device = [{"ctx": base + peer_lane, "head": peer_head} for _, peer_lane, peer_head in peers]
    sibling = {"ctx": base + flipped(lane, 1, GROUP_DEV), "head": head}
    enter(device)
    pair_copies, copies = [], []
    for step, (member, peer_lane, peer_head) in enumerate(peers):
        key_at = columns(peer_lane, peer_head)[1]
        copy = pltpu.make_async_remote_copy(
            src_ref=pair_ref.at[peer_lane % 2, :, key_at],
            dst_ref=pair_out.at[peer_lane % 2, landing, :],
            send_sem=send_sems.at[2, step],
            recv_sem=recv_sems.at[2, step],
            device_id=device[step],
            device_id_type=MESH,
        )
        copy.start()
        pair_copies.append(copy)
    for step, (member, peer_lane, peer_head) in enumerate(peers):
        query_at = columns(peer_lane, peer_head)[0]
        for index, (source, target) in enumerate(
            ((query_ref, query_out), (grad_ref, grad_out))
        ):
            copy = pltpu.make_async_remote_copy(
                src_ref=source.at[:, query_at],
                dst_ref=target.at[landing, :],
                send_sem=send_sems.at[index, step],
                recv_sem=recv_sems.at[index, step],
                device_id=device[step],
                device_id_type=MESH,
            )
            copy.start()
            copies.append(copy)
    stores = []
    for index, (stage, target) in enumerate(
        (
            (pair_stage, pair_out.at[kind, landing, :]),
            (query_stage, query_out.at[landing, :]),
            (grad_stage, grad_out.at[landing, :]),
        )
    ):
        loads[index].wait()
        store = pltpu.make_async_copy(stage, target, local_sems.at[3 + index])
        store.start()
        stores.append(store)

    def passing(slot, source, spot):
        copy = pltpu.make_async_remote_copy(
            src_ref=source,
            dst_ref=pair_out.at[kind, spot, :],
            send_sem=pass_send_sems.at[slot],
            recv_sem=pass_recv_sems.at[slot],
            device_id=sibling,
            device_id_type=MESH,
        )
        copy.start()
        return copy

    passes = [passing(members - 1, pair_stage, landing)]
    for step, (member, peer_lane, peer_head) in enumerate(peers):
        pair_copies[step].wait_recv()
        spot = rows_of(member)
        passes.append(passing(step, pair_out.at[kind, spot, :], spot))
    for store in stores:
        store.wait()
    for copy in pair_copies:
        copy.wait_send()
    for copy in copies:
        copy.wait()
    for copy in passes:
        copy.wait()


def spread(head_dim, query, grad, pair):
    rows, width = query.shape
    members = GROUP_DEV * head_dim
    wide = width // members
    any_spec = pl.BlockSpec(memory_space=pl.ANY)
    return pl.pallas_call(
        partial(spread_kernel, head_dim),
        out_shape=[
            jax.ShapeDtypeStruct((rows * members, wide), jnp.bfloat16),
            jax.ShapeDtypeStruct((rows * members, wide), jnp.bfloat16),
            jax.ShapeDtypeStruct((2, rows * members, HEAD_SIZE), jnp.bfloat16),
        ],
        in_specs=[any_spec] * 3,
        out_specs=[any_spec] * 3,
        scratch_shapes=[
            pltpu.VMEM((rows, wide), jnp.bfloat16),
            pltpu.VMEM((rows, wide), jnp.bfloat16),
            pltpu.VMEM((rows, HEAD_SIZE), jnp.bfloat16),
            pltpu.SemaphoreType.DMA((3, members - 1)),
            pltpu.SemaphoreType.DMA((3, members - 1)),
            pltpu.SemaphoreType.DMA((members,)),
            pltpu.SemaphoreType.DMA((members,)),
            pltpu.SemaphoreType.DMA((6,)),
        ],
        compiler_params=pltpu.CompilerParams(collective_id=0, has_side_effects=True),
        name="spread",
    )(query, grad, pair)


def gather_kernel(attn_ref, query_ref, pair_ref, *rest):
    attn_out, query_out, pair_out, attn_stage, query_stage, mine, other = rest[:7]
    send_sems, recv_sems, swap_sems, local_sems = rest[7:]
    rows = attn_out.shape[0]
    wide = attn_ref.shape[1]
    sharers = RATIO // (wide // HEAD_SIZE)
    ctx = lax.axis_index("ctx")
    head = lax.axis_index("head")
    base = ctx // GROUP_DEV * GROUP_DEV
    lane = ctx - base
    kind = lane % 2
    own_at = pl.ds(pl.multiple_of(lane * wide, HEAD_SIZE), wide)
    pair_at = pl.ds(pl.multiple_of(lane // sharers * HEAD_SIZE, HEAD_SIZE), HEAD_SIZE)
    pair_landing = pair_out.at[kind, lane % sharers // 2, :, pair_at]

    def taken(peer):
        return pl.ds(pl.multiple_of(peer * rows, 16), rows)

    loads = [
        pltpu.make_async_copy(pair_ref.at[kind], mine, local_sems.at[0]),
        pltpu.make_async_copy(attn_ref.at[taken(lane), :], attn_stage, local_sems.at[1]),
        pltpu.make_async_copy(query_ref.at[taken(lane), :], query_stage, local_sems.at[2]),
    ]
    for load in loads:
        load.start()
    peers = [flipped(lane, mask, GROUP_DEV) for mask in GATHER_ORDER]
    device = [{"ctx": base + peer, "head": head} for peer in peers]
    enter(device)
    swap = pltpu.make_async_remote_copy(
        src_ref=pair_ref.at[1 - kind],
        dst_ref=other,
        send_sem=swap_sems.at[0],
        recv_sem=swap_sems.at[1],
        device_id={"ctx": base + flipped(lane, 1, GROUP_DEV), "head": head},
        device_id_type=MESH,
    )
    swap.start()
    copies = []
    for step, peer in enumerate(peers):
        for index, (source, target) in enumerate(((attn_ref, attn_out), (query_ref, query_out))):
            copy = pltpu.make_async_remote_copy(
                src_ref=source.at[taken(peer), :],
                dst_ref=target.at[:, own_at],
                send_sem=send_sems.at[index, step],
                recv_sem=recv_sems.at[index, step],
                device_id=device[step],
                device_id_type=MESH,
            )
            copy.start()
            copies.append(copy)
    stores = []
    for index, (stage, target) in ((1, (attn_stage, attn_out)), (2, (query_stage, query_out))):
        loads[index].wait()
        store = pltpu.make_async_copy(stage, target.at[:, own_at], local_sems.at[2 + index])
        store.start()
        stores.append(store)
    loads[0].wait()
    swap.wait()
    for peer in range(GROUP_DEV):
        at = slice(peer * rows, (peer + 1) * rows)
        total = mine[at, :].astype(jnp.float32) + other[at, :].astype(jnp.float32)
        mine[at, :] = total.astype(jnp.bfloat16)
    store = pltpu.make_async_copy(mine.at[taken(lane), :], pair_landing, local_sems.at[5])
    store.start()
    stores.append(store)
    for step, peer in enumerate(peers):
        copy = pltpu.make_async_remote_copy(
            src_ref=mine.at[taken(peer), :],
            dst_ref=pair_landing,
            send_sem=send_sems.at[2, step],
            recv_sem=recv_sems.at[2, step],
            device_id=device[step],
            device_id_type=MESH,
        )
        copy.start()
        copies.append(copy)
    for store in stores:
        store.wait()
    for copy in copies:
        copy.wait()


GATHER_ORDER = [6, 2, 4, 7, 3, 5, 1]


def gather(attn, query, pair):
    tokens, wide = attn.shape
    rows = tokens // GROUP_DEV
    sharers = RATIO // (wide // HEAD_SIZE)
    any_spec = pl.BlockSpec(memory_space=pl.ANY)
    return pl.pallas_call(
        gather_kernel,
        out_shape=[
            jax.ShapeDtypeStruct((rows, wide * GROUP_DEV), jnp.bfloat16),
            jax.ShapeDtypeStruct((rows, wide * GROUP_DEV), jnp.bfloat16),
            jax.ShapeDtypeStruct(
                (2, sharers // 2, rows, HEAD_SIZE * GROUP_DEV // sharers), jnp.bfloat16
            ),
        ],
        in_specs=[any_spec] * 3,
        out_specs=[any_spec] * 3,
        scratch_shapes=[
            pltpu.VMEM((rows, wide), jnp.bfloat16),
            pltpu.VMEM((rows, wide), jnp.bfloat16),
            pltpu.VMEM((tokens, HEAD_SIZE), jnp.bfloat16),
            pltpu.VMEM((tokens, HEAD_SIZE), jnp.bfloat16),
            pltpu.SemaphoreType.DMA((3, GROUP_DEV - 1)),
            pltpu.SemaphoreType.DMA((3, GROUP_DEV - 1)),
            pltpu.SemaphoreType.DMA((2,)),
            pltpu.SemaphoreType.DMA((6,)),
        ],
        compiler_params=pltpu.CompilerParams(collective_id=1, has_side_effects=True),
        name="gather",
    )(attn, query, pair)


def dot(left, right):
    return jnp.dot(left, right, preferred_element_type=jnp.float32)


def attend_kernel(
    firsts_ref,
    places_ref,
    query_ref,
    grad_ref,
    pair_ref,
    attn_ref,
    query_grad_ref,
    pair_grad_ref,
    keys,
    values,
    keys_t,
    values_t,
    store,
    out_t,
    query_grad_t,
    key_total,
    value_total,
):
    heads = query_ref.shape[1] // HEAD_SIZE
    block = MASK_BLOCK_SIZE
    columns = heads * block
    half = SPAN_TOKENS // 2
    scale = HEAD_SIZE ** (-0.5)
    scale_log2 = scale * math.log2(math.e)
    tail = keys.shape[0] - SPAN_TOKENS
    for kind, flat, turned in ((0, keys, keys_t), (1, values, values_t)):
        flat[0:half, :] = pair_ref[kind, half:SPAN_TOKENS, :]
        flat[half:SPAN_TOKENS, :] = pair_ref[kind, 0:half, :]
        flat[SPAN_TOKENS:, :] = jnp.zeros((tail, HEAD_SIZE), jnp.bfloat16)
        turned[:, SPAN_TOKENS:] = jnp.zeros((HEAD_SIZE, tail), jnp.bfloat16)
    for index in range(GROUP_BLOCKS):
        at = slice(index * block, (index + 1) * block)
        keys_t[:, at] = keys[at, :].T
        values_t[:, at] = values[at, :].T
    key_total[...] = jnp.zeros_like(key_total)
    value_total[...] = jnp.zeros_like(value_total)
    token = lax.rem(lax.broadcasted_iota(jnp.int32, (CHUNK, columns), 1), block)
    key_at = lax.broadcasted_iota(jnp.int32, (CHUNK, columns), 0)
    ahead = key_at - token

    def one_block(index, _):
        first = firsts_ref[index]
        count = index - first + 1
        steps = (count * block + CHUNK - 1) // CHUNK
        loader = lax.rem(index + GROUP_BLOCKS // 2, GROUP_BLOCKS)
        source = pl.ds(pl.multiple_of(loader * block, block), block)
        target = pl.ds(pl.multiple_of(places_ref[loader] * block, block), block)
        parts = [slice(h * HEAD_SIZE, (h + 1) * HEAD_SIZE) for h in range(heads)]
        query = jnp.concatenate([query_ref[source, at] for at in parts], axis=0)
        grad = jnp.concatenate([grad_ref[source, at] for at in parts], axis=0)
        query_t = jnp.concatenate([query_ref[source, at].T for at in parts], axis=1)
        grad_t = jnp.concatenate([grad_ref[source, at].T for at in parts], axis=1)

        def spot(step):
            return pl.ds(pl.multiple_of(first * block + step * CHUNK, block), CHUNK)

        def slot(step):
            return pl.ds(pl.multiple_of(step * CHUNK, CHUNK), CHUNK)

        def logits(step, peak):
            raw = dot(keys[spot(step), :], query_t)
            bound = (count - 1) * block - step * CHUNK
            raw = jnp.where(ahead <= bound, raw, MASKED_LOGIT)
            store[slot(step), :] = raw
            return jnp.maximum(peak, jnp.max(raw, axis=0, keepdims=True))

        peak = lax.fori_loop(
            0, steps, logits, jnp.full((1, columns), MASKED_LOGIT, jnp.float32)
        )
        peak = peak * scale_log2
        out_t[...] = jnp.zeros_like(out_t)

        def mix(step, total):
            mass = jnp.exp2(store[slot(step), :] * scale_log2 - peak)
            store[slot(step), :] = mass
            out_t[...] += dot(values_t[:, spot(step)], mass.astype(jnp.bfloat16))
            return total + jnp.sum(mass, axis=0, keepdims=True)

        total = lax.fori_loop(0, steps, mix, jnp.zeros((1, columns), jnp.float32))
        share = 1.0 / total
        out = (out_t[...] * share).astype(jnp.bfloat16)
        delta = jnp.sum(
            out.astype(jnp.float32) * grad_t.astype(jnp.float32), axis=0, keepdims=True
        )
        for h, at in enumerate(parts):
            attn_ref[target, at] = out[:, h * block : (h + 1) * block].T
        query_grad_t[...] = jnp.zeros_like(query_grad_t)

        def back(step, carry):
            weights = store[slot(step), :] * share
            value_total[spot(step), :] += dot(weights.astype(jnp.bfloat16), grad)
            grad_weights = dot(values[spot(step), :], grad_t)
            dlogits = (weights * (grad_weights - delta)).astype(jnp.bfloat16)
            key_total[spot(step), :] += dot(dlogits, query)
            query_grad_t[...] += dot(keys_t[:, spot(step)], dlogits)
            return carry

        lax.fori_loop(0, steps, back, 0)
        moved = (query_grad_t[...] * scale).astype(jnp.bfloat16)
        for h, at in enumerate(parts):
            query_grad_ref[target, at] = moved[:, h * block : (h + 1) * block].T
        return 0

    lax.fori_loop(0, GROUP_BLOCKS, one_block, 0)

    def finish(index, _):
        loader = lax.rem(index + GROUP_BLOCKS // 2, GROUP_BLOCKS)
        source = pl.ds(pl.multiple_of(index * block, block), block)
        target = pl.ds(pl.multiple_of(places_ref[loader] * block, block), block)
        pair_grad_ref[0, target, :] = (key_total[source, :] * scale).astype(jnp.bfloat16)
        pair_grad_ref[1, target, :] = value_total[source, :].astype(jnp.bfloat16)
        return 0

    lax.fori_loop(0, GROUP_BLOCKS, finish, 0)


def attend(firsts, places, query, grad, pair):
    wide = query.shape[1]
    columns = wide // HEAD_SIZE * MASK_BLOCK_SIZE
    padded = SPAN_TOKENS + CHUNK - MASK_BLOCK_SIZE
    vmem = pl.BlockSpec(memory_space=pltpu.VMEM)
    smem = pl.BlockSpec(memory_space=pltpu.SMEM)
    return pl.pallas_call(
        attend_kernel,
        out_shape=[
            jax.ShapeDtypeStruct(query.shape, jnp.bfloat16),
            jax.ShapeDtypeStruct(query.shape, jnp.bfloat16),
            jax.ShapeDtypeStruct(pair.shape, jnp.bfloat16),
        ],
        in_specs=[smem, smem, vmem, vmem, vmem],
        out_specs=[vmem] * 3,
        scratch_shapes=[
            pltpu.VMEM((padded, HEAD_SIZE), jnp.bfloat16),
            pltpu.VMEM((padded, HEAD_SIZE), jnp.bfloat16),
            pltpu.VMEM((HEAD_SIZE, padded), jnp.bfloat16),
            pltpu.VMEM((HEAD_SIZE, padded), jnp.bfloat16),
            pltpu.VMEM((MOST * MASK_BLOCK_SIZE, columns), jnp.float32),
            pltpu.VMEM((HEAD_SIZE, columns), jnp.float32),
            pltpu.VMEM((HEAD_SIZE, columns), jnp.float32),
            pltpu.VMEM((padded, HEAD_SIZE), jnp.float32),
            pltpu.VMEM((padded, HEAD_SIZE), jnp.float32),
        ],
        compiler_params=pltpu.CompilerParams(vmem_limit_bytes=60 * 1024 * 1024),
        name="attend",
    )(firsts, places, query, grad, pair)


def body(head_dim, query_rows, key_rows, value_rows, grad_rows, doc_blocks, block_perm):
    group = lax.axis_index("ctx") // GROUP_DEV
    firsts = doc_first(lax.dynamic_index_in_dim(doc_blocks, group, 0, keepdims=False))
    places = lax.dynamic_slice_in_dim(block_perm, group * GROUP_BLOCKS, GROUP_BLOCKS)
    places = places - group * GROUP_BLOCKS
    query, grad, pair = spread(head_dim, query_rows, grad_rows, jnp.stack([key_rows, value_rows]))
    attn, query_grad, parts = gather(*attend(firsts, places, query, grad, pair))
    if parts.shape[1] > 1:
        parts = jnp.sum(parts.astype(jnp.float32), axis=1).astype(jnp.bfloat16)
    else:
        parts = parts[:, 0]
    return attn, query_grad, parts[0], parts[1]


def solution(mesh):
    split = P(("ctx", "head"), None)
    out_spec = P("ctx", "head")
    return jax.shard_map(
        partial(body, mesh.shape["head"]),
        mesh=mesh,
        in_specs=(split, split, split, split, P(), P()),
        out_specs=(out_spec,) * 4,
        check_vma=False,
    )
```
